32 devices in a mesh: fsdp: 2 (over x), ctx: 4 (over y, core), tp: 4 (over z).
Axes of the slice: x: 2, y: 2, z: 4, core: 2. Of those that a mesh axis runs over, the one named last changes fastest.
Arguments:
- block_in: bfloat16 [8, 1024, 2048], P('fsdp', 'ctx', 'tp'), may hold values from -6 to 6
- seg_ids: int32 [8, 1024], P('fsdp'), may hold values from 0 to 7, never falling along the last dimension, each value on 1 to 512 neighbouring positions
- out_cot: bfloat16 [8, 1024, 2048], P('fsdp', 'ctx'), may hold values from -6 to 6
- norm_gain: bfloat16 [2048], P('tp'), may hold values from 0.099609375 to 1.8984375
- mid_gain: bfloat16 [2048], P('tp'), may hold values from 0.099609375 to 1.8984375
- gelu_proj: bfloat16 [2048, 2816], P(('fsdp', 'ctx'), 'tp'), may hold values from -0.125 to 0.125
- scan_proj: bfloat16 [2048, 2816], P(('fsdp', 'ctx'), 'tp'), may hold values from -0.125 to 0.125
- out_proj: bfloat16 [2816, 2048], P('tp', ('fsdp', 'ctx')), may hold values from -0.4375 to 0.4375
- gate_proj: bfloat16 [2048, 6144], P(('fsdp', 'ctx'), 'tp'), may hold values from -0.125 to 0.125
- up_proj: bfloat16 [2048, 6144], P(('fsdp', 'ctx'), 'tp'), may hold values from -0.125 to 0.125
- down_proj: bfloat16 [6144, 2048], P('tp', ('fsdp', 'ctx')), may hold values from -0.109375 to 0.109375
- conv_kernel: float32 [4, 2816], P(None, 'tp'), may hold values from -3 to 3
- conv_bias: float32 [2816], P('tp'), may hold values from -3 to 3
- rate_gate: bfloat16 [16, 176, 176], P('tp'), may hold values from -0.4375 to 0.4375
- input_gate: bfloat16 [16, 176, 176], P('tp'), may hold values from -0.4375 to 0.4375
- rate_bias: float32 [2816], P('tp'), may hold values from -4 to 4
- input_bias: float32 [2816], P('tp'), may hold values from -4 to 4
- decay_param: float32 [2816], P('tp'), may hold values from -16 to -4
Outputs:
- block_out: bfloat16 [8, 1024, 2048], P('fsdp', 'ctx', 'tp')
- grad_in: float32 [8, 1024, 2048], P('fsdp', 'ctx', 'tp')
- grad_norm_gain: float32 [2048], P('tp')
- grad_mid_gain: float32 [2048], P('tp')
- grad_gelu_proj: float32 [2048, 2816], P(('fsdp', 'ctx'), 'tp')
- grad_scan_proj: float32 [2048, 2816], P(('fsdp', 'ctx'), 'tp')
- grad_out_proj: float32 [2816, 2048], P('tp', ('fsdp', 'ctx'))
- grad_gate_proj: float32 [2048, 6144], P(('fsdp', 'ctx'), 'tp')
- grad_up_proj: float32 [2048, 6144], P(('fsdp', 'ctx'), 'tp')
- grad_down_proj: float32 [6144, 2048], P('tp', ('fsdp', 'ctx'))
- grad_conv_kernel: float32 [4, 2816], P(None, 'tp')
- grad_conv_bias: float32 [2816], P('tp')
- grad_rate_gate: float32 [16, 176, 176], P('tp')
- grad_input_gate: float32 [16, 176, 176], P('tp')
- grad_rate_bias: float32 [2816], P('tp')
- grad_input_bias: float32 [2816], P('tp')
- grad_decay_param: float32 [2816], P('tp')
The draws below stay inside these ranges and needn't reach their ends.
Inputs may be any that keep to these rules, and one draw needn't show every extreme that they name: `seg_ids`: in every row the document numbers never fall; each of the 8 documents covers 1 to 512 positions, and one covers exactly 512.
All inputs are finite; a program needn't handle non-finite values.
Results may differ from the reference program's by a relative error of at most 0.0095.
Values may be sent and summed in bfloat16 or wider, within the bound.
A program may use at most 320 MiB of HBM per device.

```python
import math
import jax
import jax.numpy as jnp
import numpy as np
from jax import lax

D = 2048
HEADS = 16
HS = 176
FF = 6144
CONV = 4
DOCS = 8
R = 2816
LENGTH = 1024
BATCH = 8


def draw_decay_param(key, part):
    upper_end = LENGTH / 20.0
    fraction = jax.random.uniform(key, (R,), jnp.float32)
    spans = jnp.exp(jnp.log(0.05) + fraction * (jnp.log(upper_end) - jnp.log(0.05)))
    return jnp.log(jnp.expm1(spans / (4.0 * LENGTH)))


def level_of(key, dims, cuts, least, top_value):
    gain, own = 1.0, jax.random.fold_in(key, 6)
    for dim, parts in cuts:
        heights = jnp.exp(jax.random.uniform(jax.random.fold_in(own, dim), (parts,), jnp.float32, least / len(cuts), top_value / len(cuts)))
        gain = gain * jnp.repeat(heights, dims[dim] // parts).reshape([-1 if axis == dim else 1 for axis in range(len(dims))])
    return gain


def split_up(count, total, most, slope):
    portions = [(1 << 20) // math.isqrt(rank ** slope) + 1 for rank in range(2, count + 1)]
    rest, holding = total - most - (count - 1), [1] * (count - 1)
    while rest > 0:
        movable = [i for i in range(count - 1) if holding[i] < most]
        mass, left = sum([portions[i] for i in movable]), rest
        for i in movable:
            more = min(most - holding[i], max(1, left * portions[i] // mass), rest)
            holding[i] = holding[i] + more
            rest = rest - more
    return np.array([most] + holding)


def ragged(key, amount, total, most, skew):
    if amount == 2:
        one = jax.random.randint(key, (), max(1, total - most), min(most, total - 1) + 1)
        return jnp.stack([one, total - one])
    tallies = jnp.asarray(split_up(amount, total, most, skew), jnp.int32)
    couples = (amount - 1) // 2
    source_of, sink = tallies[1:1 + 2 * couples:2], tallies[2:2 + 2 * couples:2]
    margin = jnp.minimum(source_of - 1, most - sink)
    moved = jax.random.randint(jax.random.fold_in(key, 1), (couples,), 0, 1 << 20) % (margin + 1)
    tallies = tallies.at[1:1 + 2 * couples:2].set(source_of - moved).at[2:2 + 2 * couples:2].set(sink + moved)
    return tallies[jax.random.permutation(jax.random.fold_in(key, 2), amount)]


def bell_draw(stream_key, shape, deviation, bound, shards=(), held_as=jnp.bfloat16):
    values = deviation * jax.random.normal(stream_key, shape, jnp.float32)
    if shards:
        values = values * level_of(stream_key, shape, shards, -0.22, 0.18)
    return jnp.clip(values, -bound, bound).astype(held_as)


def setup_inputs(seed: int = 0) -> dict:
    key_list = jax.random.split(jax.random.key(seed), 19)
    block_in = bell_draw(key_list[0], (BATCH, LENGTH, D), 1.0, 6.0, ((0, 2), (1, 4), (2, 4)))
    seg_ids = jax.vmap(lambda own: jnp.searchsorted(jnp.cumsum(ragged(own, DOCS, LENGTH, LENGTH // 2, 2)), jnp.arange(LENGTH), side="right"))(jax.random.split(key_list[1], BATCH)).reshape((BATCH, LENGTH)).astype(jnp.int32)
    out_cot = bell_draw(key_list[2], (BATCH, LENGTH, D), 1.0, 6.0, ((0, 2), (1, 4)))
    norm_gain = jnp.clip(1.0 + 0.18 * jax.random.normal(key_list[3], (D,), jnp.float32), 0.099609375, 1.8984375).astype(jnp.bfloat16)
    mid_gain = jnp.clip(1.0 + 0.18 * jax.random.normal(key_list[4], (D,), jnp.float32), 0.099609375, 1.8984375).astype(jnp.bfloat16)
    gelu_proj = bell_draw(key_list[5], (D, R), D ** -0.5, 0.125, ((0, 8), (1, 4)))
    scan_proj = bell_draw(key_list[6], (D, R), D ** -0.5, 0.125, ((0, 8), (1, 4)))
    out_proj = bell_draw(key_list[7], (R, D), (R // 16) ** -0.5, 0.4375, ((0, 4), (1, 8)))
    gate_proj = bell_draw(key_list[8], (D, FF), D ** -0.5, 0.125, ((0, 8), (1, 4)))
    up_proj = bell_draw(key_list[9], (D, FF), D ** -0.5, 0.125, ((0, 8), (1, 4)))
    down_proj = bell_draw(key_list[10], (FF, D), (FF // 2) ** -0.5, 0.109375, ((0, 4), (1, 8)))
    conv_kernel = bell_draw(key_list[11], (CONV, R), CONV ** -0.5, 3.0, ((1, 4),), jnp.float32)
    conv_bias = bell_draw(key_list[12], (R,), 0.5, 3.0, ((0, 4),), jnp.float32)
    rate_gate = bell_draw(key_list[13], (HEADS, HS, HS), HS ** -0.5, 0.4375, ((0, 4),))
    input_gate = bell_draw(key_list[14], (HEADS, HS, HS), HS ** -0.5, 0.4375, ((0, 4),))
    rate_bias = bell_draw(key_list[15], (R,), 1.0, 4.0, ((0, 4),), jnp.float32)
    input_bias = bell_draw(key_list[16], (R,), 1.0, 4.0, ((0, 4),), jnp.float32)
    decay_param = draw_decay_param(jax.random.fold_in(key_list[18], 71), 0)
    return dict(block_in=block_in, seg_ids=seg_ids, out_cot=out_cot, norm_gain=norm_gain, mid_gain=mid_gain, gelu_proj=gelu_proj, scan_proj=scan_proj, out_proj=out_proj, gate_proj=gate_proj, up_proj=up_proj, down_proj=down_proj, conv_kernel=conv_kernel, conv_bias=conv_bias, rate_gate=rate_gate, input_gate=input_gate, rate_bias=rate_bias, input_bias=input_bias, decay_param=decay_param)


@jax.custom_vjp
def low(v):
    return lax.optimization_barrier(v.astype(jnp.bfloat16)).astype(jnp.float32)

@jax.custom_vjp
def low_back(v):
    return v

def low_keep(v):
    return (low(v), None)

def low_pass(kept, grad):
    return (grad,)

def back_keep(v):
    return (v, None)

def back_low(kept, grad):
    return (low(grad),)
low.defvjp(low_keep, low_pass)
low_back.defvjp(back_keep, back_low)
eps_norm = 1e-06

def rms_scale(values, gain_vec):
    return values * lax.rsqrt(lax.optimization_barrier(jnp.mean(values * values, axis=-1, keepdims=True)) + eps_norm) * gain_vec

def gelu_tanh(values):
    return jax.nn.gelu(values, approximate=True)

def gate_values(pre_rate, pre_input, decay_param):
    rate_vals = jax.nn.sigmoid(pre_rate)
    input_vals = jax.nn.sigmoid(pre_input)
    log_a = -8.0 * jax.nn.softplus(decay_param) * rate_vals
    return (jnp.exp(log_a), jnp.sqrt(-jnp.expm1(2.0 * log_a)) * input_vals)

def matmul(left, right):
    return jnp.dot(left, right, precision=lax.Precision.HIGHEST)

def block_forward(seg_ids, block_in, norm_gain, mid_gain, gelu_proj, scan_proj, out_proj, gate_proj, up_proj, down_proj, conv_kernel, conv_bias, rate_gate, input_gate, rate_bias, input_bias, decay_param):
    seq_count, seq_len, model_dim = block_in.shape
    rec_dim = gelu_proj.shape[1]
    normed = low(rms_scale(block_in, norm_gain))
    y_pre = low_back(matmul(normed, gelu_proj))
    x_branch = low(low_back(matmul(normed, scan_proj)))
    margin_len = CONV - 1
    padded_ids = jnp.concatenate([jnp.full((seq_count, margin_len), -1, jnp.int32), seg_ids.astype(jnp.int32)], axis=1)
    padded_x = jnp.concatenate([jnp.zeros((seq_count, margin_len, rec_dim), jnp.float32), x_branch], axis=1)
    conv_sum = conv_bias + jnp.zeros((seq_count, seq_len, rec_dim), jnp.float32)
    for offset in range(CONV):
        same_doc = (padded_ids[:, margin_len - offset:margin_len - offset + seq_len] == seg_ids).astype(jnp.float32)
        conv_sum = conv_sum + conv_kernel[offset] * padded_x[:, margin_len - offset:margin_len - offset + seq_len] * same_doc[..., None]
    conv_out = low(low_back(conv_sum))
    heads_in = conv_out.reshape(seq_count, seq_len, HEADS, HS)
    pre_rate = low_back(jnp.einsum('bthi,hij->bthj', heads_in, rate_gate, precision=lax.Precision.HIGHEST).reshape(seq_count, seq_len, rec_dim) + rate_bias)
    pre_input = low_back(jnp.einsum('bthi,hij->bthj', heads_in, input_gate, precision=lax.Precision.HIGHEST).reshape(seq_count, seq_len, rec_dim) + input_bias)
    decays, in_scale = gate_values(pre_rate, pre_input, decay_param)
    keep_state = (padded_ids[:, margin_len - 1:margin_len - 1 + seq_len] == seg_ids).astype(jnp.float32)
    coeffs = decays * keep_state[..., None]
    inputs = in_scale * conv_out

    def advance(carry_state, pair_in):
        new_state = pair_in[0] * carry_state + pair_in[1]
        return (new_state, new_state)
    _, states = lax.scan(advance, jnp.zeros((seq_count, rec_dim), jnp.float32), (jnp.swapaxes(coeffs, 0, 1), jnp.swapaxes(inputs, 0, 1)))
    states = jnp.swapaxes(states, 0, 1)
    mixed_in = low(states * gelu_tanh(y_pre))
    mid_res = block_in + low_back(matmul(mixed_in, out_proj))
    normed_mid = low(rms_scale(mid_res, mid_gain))
    gate_pre = low_back(matmul(normed_mid, gate_proj))
    up_pre = low_back(matmul(normed_mid, up_proj))
    hidden = low(gelu_tanh(gate_pre) * up_pre)
    return mid_res + low_back(matmul(hidden, down_proj))

def reference(block_in, seg_ids, out_cot, norm_gain, mid_gain, gelu_proj, scan_proj, out_proj, gate_proj, up_proj, down_proj, conv_kernel, conv_bias, rate_gate, input_gate, rate_bias, input_bias, decay_param):
    floats = (block_in, norm_gain, mid_gain, gelu_proj, scan_proj, out_proj, gate_proj, up_proj, down_proj, conv_kernel, conv_bias, rate_gate, input_gate, rate_bias, input_bias, decay_param)
    floats = tuple((item.astype(jnp.float32) for item in floats))

    def forward_only(*params):
        return block_forward(seg_ids, *params)
    result, back_fn = jax.vjp(forward_only, *floats)
    grads = back_fn(out_cot.astype(jnp.float32))
    return (result.astype(jnp.bfloat16), grads[0], grads[1], grads[2], grads[3], grads[4], grads[5], grads[6], grads[7], grads[8], grads[9], grads[10], grads[11], grads[12], grads[13], grads[14], grads[15])
```

```python
import functools

import jax
import jax.numpy as jnp
from jax import lax
from jax.experimental import pallas as pl
from jax.experimental.pallas import tpu as pltpu
from jax.sharding import PartitionSpec as P

CONV = 4
EPS = 1e-06
LANES = 128
SEGS = 8
F32 = jnp.float32
BF16 = jnp.bfloat16


def xor_permute(value, axis, bit):
    count = lax.axis_size(axis)
    return lax.ppermute(value, axis, [(i, i ^ bit) for i in range(count)])


def quad_mesh():
    return lax.axis_size("fsdp") == 2 and lax.axis_size("ctx") == 4


def own_place():
    place = lax.axis_index("ctx")
    return lax.axis_index("fsdp"), place // 2, place % 2


def gather_rows(shard):
    rows, width = shard.shape
    if not quad_mesh():
        return lax.all_gather(shard, ("fsdp", "ctx"), axis=0, tiled=True)
    half = rows // 2
    own_x, own_y, own_c = own_place()
    from_x = xor_permute(shard, "fsdp", 1)
    from_y = xor_permute(shard, "ctx", 2)
    corner_top = xor_permute(from_y[:half], "fsdp", 1)
    corner_low = xor_permute(from_x[half:], "ctx", 2)
    quad = jnp.zeros((2, 2, rows, width), shard.dtype)

    def place(buffer, block, at_x, at_y, row):
        return lax.dynamic_update_slice(buffer, block[None, None], (at_x, at_y, row, 0))

    quad = place(quad, shard, own_x, own_y, 0)
    quad = place(quad, from_x, 1 - own_x, own_y, 0)
    quad = place(quad, from_y, own_x, 1 - own_y, 0)
    quad = place(quad, corner_top, 1 - own_x, 1 - own_y, 0)
    quad = place(quad, corner_low, 1 - own_x, 1 - own_y, half)
    quad = quad.reshape(4, 1, rows, width)
    other = xor_permute(quad, "ctx", 1)
    full = jnp.zeros((4, 2, rows, width), shard.dtype)
    full = lax.dynamic_update_slice(full, quad, (0, own_c, 0, 0))
    full = lax.dynamic_update_slice(full, other, (0, 1 - own_c, 0, 0))
    return full.reshape(8 * rows, width)


def pick(value, index, axis):
    return lax.dynamic_index_in_dim(value, index, axis, keepdims=False)


def add_low(left, right):
    return (left.astype(F32) + right.astype(F32)).astype(BF16)


def scatter_rows(partial):
    if not quad_mesh():
        return lax.psum_scatter(
            partial, ("fsdp", "ctx"), scatter_dimension=0, tiled=True
        ).astype(F32)
    total, width = partial.shape
    rows = total // 8
    half = rows // 2
    own_x, own_y, own_c = own_place()
    cube = partial.reshape(4, 2, rows, width)
    got = xor_permute(pick(cube, 1 - own_c, 1), "ctx", 1)
    quad = add_low(pick(cube, own_c, 1), got).reshape(2, 2, rows, width)
    top, low = quad[:, :, :half], quad[:, :, half:]
    top_got = xor_permute(pick(top, 1 - own_x, 0), "fsdp", 1)
    low_got = xor_permute(pick(low, 1 - own_y, 1), "ctx", 2)
    top = add_low(pick(top, own_x, 0), top_got)
    low = add_low(pick(low, own_y, 1), low_got)
    top_last = xor_permute(pick(top, 1 - own_y, 0), "ctx", 2)
    low_last = xor_permute(pick(low, 1 - own_x, 0), "fsdp", 1)
    top = pick(top, own_y, 0).astype(F32) + top_last.astype(F32)
    low = pick(low, own_x, 0).astype(F32) + low_last.astype(F32)
    return jnp.concatenate([top, low], axis=0)


def total_over_tokens(value):
    if not quad_mesh():
        return lax.psum(value, ("fsdp", "ctx"))
    value = value + xor_permute(value, "ctx", 1)
    value = value + xor_permute(value, "fsdp", 1)
    return value + xor_permute(value, "ctx", 2)


def from_behind(value, axis, steps):
    count = lax.axis_size(axis)
    leading, last = (max(0, -steps), min(count, count - steps))
    return lax.ppermute(value, axis, [(source, source + steps) for source in range(leading, last)])


def entering(coef, state, backward):
    count, mine = lax.axis_size("ctx"), lax.axis_index("ctx")
    both = lax.all_gather(jnp.stack([coef, state]), "ctx")
    total = jnp.zeros_like(state)
    for step in range(count - 1):
        position = count - 1 - step if backward else step
        before = position > mine if backward else position < mine
        total = jnp.where(before, both[position, 0] * total + both[position, 1], total)
    return total


def dot_nt(left, right):
    return lax.dot_general(left, right, (((1,), (1,)), ((), ())), preferred_element_type=F32)


def dot_tn(left, right):
    return lax.dot_general(left, right, (((0,), (0,)), ((), ())), preferred_element_type=F32)


def dot_nn(left, right):
    return jnp.dot(left, right, preferred_element_type=F32)


GELU_C = 0.7978845608028654
GELU_A = 0.044715


def gelu_parts(values):
    square = values * values
    tanh = jnp.tanh(GELU_C * values * (1.0 + GELU_A * square))
    act = 0.5 * values * (1.0 + tanh)
    slope = 0.5 * (1.0 + tanh) + 0.5 * values * (1.0 - tanh * tanh) * GELU_C * (
        1.0 + 3.0 * GELU_A * square
    )
    return act, slope


def minus_expm1(value):
    series = 1.0 / 40320.0
    for factor in (5040.0, 720.0, 120.0, 24.0, 6.0, 2.0, 1.0):
        series = series * value + 1.0 / factor
    return jnp.where(value > -0.5, -value * series, 1.0 - jnp.exp(value))


def softplus(value):
    return jnp.maximum(value, 0.0) + jnp.log1p(jnp.exp(-jnp.abs(value)))


def sigmoid(value):
    return 1.0 / (1.0 + jnp.exp(-value))


def chunked(total, size, body):
    def step(index, carry):
        body(pl.multiple_of(index * size, size))
        return carry

    lax.fori_loop(0, total // size, step, 0)


def scan_rows(coef_tiles, value_tiles, coef_ref, value_ref, backward):
    tiles, rows, lanes = value_tiles.shape
    part = rows // SEGS

    def step(index, carry):
        at = part - 1 - index if backward else index
        rows_at = pl.ds(at, SEGS, stride=part)
        out = []
        for tile, (coef_run, value_run) in enumerate(carry):
            coef = coef_tiles[tile, rows_at, :]
            value_run = coef * value_run + value_tiles[tile, rows_at, :]
            coef_run = coef * coef_run
            coef_tiles[tile, rows_at, :] = coef_run
            value_tiles[tile, rows_at, :] = value_run
            out.append((coef_run, value_run))
        return tuple(out)

    start = (jnp.ones((SEGS, lanes), F32), jnp.zeros((SEGS, lanes), F32))
    ends = lax.fori_loop(0, part, step, (start,) * tiles)
    order = list(range(SEGS))[::-1] if backward else list(range(SEGS))
    for tile, (coef_end, value_end) in enumerate(ends):
        columns = slice(tile * lanes, (tile + 1) * lanes)
        coef_in, value_in = jnp.ones((1, lanes), F32), jnp.zeros((1, lanes), F32)
        for seg in order:
            window = pl.ds(seg * part, part)
            coef = coef_tiles[tile, window, :]
            value_ref[window, columns] = value_tiles[tile, window, :] + coef * value_in
            coef_ref[window, columns] = coef * coef_in
            value_in = coef_end[seg : seg + 1] * value_in + value_end[seg : seg + 1]
            coef_in = coef_end[seg : seg + 1] * coef_in


def shifted(ref, at, count, offset):
    if offset % 8 == 0:
        return ref[pl.ds(at + offset, count), :]
    return ref[pl.ds(at, count + 8), :][offset : offset + count]


def put_tiles(tiles_ref, window, value):
    for tile in range(tiles_ref.shape[0]):
        tiles_ref[tile, window, :] = value[:, tile * LANES : (tile + 1) * LANES]


def forward_kernel(
    x_ref, edge_ref, mask_ref, vec_ref, gate_ref,
    conv_ref, rate_ref, input_ref, coef_ref, state_ref,
    ext, pre, coef_tiles, value_tiles,
):
    rows, width = x_ref.shape
    ext[0:8, :] = edge_ref[...].astype(F32)
    ext[8:, :] = x_ref[...].astype(F32)
    chunk = 32

    def conv(at):
        total = vec_ref[4:5, :]
        for tap in range(CONV):
            total = total + vec_ref[tap : tap + 1, :] * shifted(ext, at, chunk, 8 - tap) * mask_ref[
                pl.ds(at, chunk), tap : tap + 1
            ]
        conv_ref[pl.ds(at, chunk), :] = total.astype(BF16)

    chunked(rows, chunk, conv)
    pre[...] = dot_nn(conv_ref[...], gate_ref[...])
    decay = -8.0 * softplus(vec_ref[7:8, :])

    def gates(at):
        window = pl.ds(at, chunk)
        rate = sigmoid(pre[window, :width] + vec_ref[5:6, :])
        gate = sigmoid(pre[window, width:] + vec_ref[6:7, :])
        log_a = decay * rate
        rate_ref[window, :] = rate
        input_ref[window, :] = gate
        put_tiles(coef_tiles, window, jnp.exp(log_a) * mask_ref[window, 1:2])
        put_tiles(
            value_tiles, window, jnp.sqrt(minus_expm1(2.0 * log_a)) * gate * conv_ref[window, :].astype(F32)
        )

    chunked(rows, chunk, gates)
    scan_rows(coef_tiles, value_tiles, coef_ref, state_ref, False)


def forward_call(x_branch, edge, masks, vectors, gates):
    count, rows, width = x_branch.shape
    seq = lambda *tail: pl.BlockSpec((None, *tail), lambda i: (i, 0, 0))
    whole = lambda *shape: pl.BlockSpec(shape, lambda i: (0, 0))
    wide = jax.ShapeDtypeStruct((count, rows, width), F32)
    return pl.pallas_call(
        forward_kernel,
        grid=(count,),
        in_specs=[
            seq(rows, width), seq(8, width), seq(rows, LANES), whole(8, width), whole(width, 2 * width)
        ],
        out_specs=[seq(rows, width)] * 5,
        out_shape=[jax.ShapeDtypeStruct((count, rows, width), BF16), wide, wide, wide, wide],
        scratch_shapes=[
            pltpu.VMEM((rows + 8, width), F32),
            pltpu.VMEM((rows, 2 * width), F32),
            pltpu.VMEM((width // LANES, rows, LANES), F32),
            pltpu.VMEM((width // LANES, rows, LANES), F32),
        ],
        cost_estimate=pl.CostEstimate(
            flops=4 * count * rows * width * width,
            bytes_accessed=count * rows * width * 20,
            transcendentals=count * rows * width * 6,
        ),
        name="conv_gates_scan",
    )(x_branch, edge, masks, vectors, gates)


def reverse_kernel(
    grad_ref, y_ref, state_ref, rate_ref, mask_ref, vec_ref, y_grad_ref, direct_ref, coef_ref, value_ref,
    coef_tiles, value_tiles,
):
    rows, width = grad_ref.shape
    decay = -8.0 * softplus(vec_ref[7:8, :])

    def body(at):
        window = pl.ds(at, 32)
        act, slope = gelu_parts(y_ref[window, :])
        grad = grad_ref[window, :]
        y_grad_ref[window, :] = (grad * state_ref[window, :] * slope).astype(BF16)
        direct = grad * act
        coef = jnp.exp(decay * rate_ref[window, :]) * mask_ref[window, 1:2]
        direct_ref[window, :] = direct
        put_tiles(coef_tiles, window, coef)
        put_tiles(value_tiles, window, coef * direct)

    chunked(rows, 32, body)
    scan_rows(coef_tiles, value_tiles, coef_ref, value_ref, True)


def reverse_call(grad, y_pre, states, rate, masks, vectors):
    count, rows, width = grad.shape
    seq = lambda *tail: pl.BlockSpec((None, *tail), lambda i: (i, 0, 0))
    whole = lambda *shape: pl.BlockSpec(shape, lambda i: (0, 0))
    wide = jax.ShapeDtypeStruct((count, rows, width), F32)
    return pl.pallas_call(
        reverse_kernel,
        grid=(count,),
        in_specs=[seq(rows, width)] * 4 + [seq(rows, LANES), whole(8, width)],
        out_specs=[seq(rows, width)] * 4,
        out_shape=[jax.ShapeDtypeStruct((count, rows, width), BF16), wide, wide, wide],
        scratch_shapes=[pltpu.VMEM((width // LANES, rows, LANES), F32)] * 2,
        cost_estimate=pl.CostEstimate(
            flops=40 * count * rows * width,
            bytes_accessed=count * rows * width * 30,
            transcendentals=count * rows * width * 2,
        ),
        name="reverse_scan",
    )(grad, y_pre, states, rate, masks, vectors)


def backward_kernel(
    direct_ref, coef_ref, value_ref, enter_ref, state_ref, before_ref, rate_ref, input_ref, conv_ref,
    x_ref, edge_ref, mask_ref, ahead_ref, vec_ref, gate_ref,
    branch_ref, tail_ref, head_ref, sums_ref, gate_grad_ref,
    ext, states, value, both, conv_grad,
):
    rows, width = direct_ref.shape
    chunk = 32
    decay = -8.0 * softplus(vec_ref[7:8, :])
    lean = -8.0 * sigmoid(vec_ref[7:8, :])
    first = pl.program_id(0) == 0

    ext[0:8, :] = edge_ref[...].astype(F32)
    ext[8:, :] = x_ref[...].astype(F32)
    states[7:8, :] = before_ref[0:1, :]
    states[8:, :] = state_ref[...]
    value[0:rows, :] = value_ref[...] + coef_ref[...] * enter_ref[0:1, :]
    value[rows : rows + 1, :] = enter_ref[0:1, :]

    @pl.when(first)
    def _():
        sums_ref[...] = jnp.zeros_like(sums_ref)

    zero = jnp.zeros((8, width), F32)

    def fold(array):
        return array.reshape(chunk // 8, 8, width).sum(axis=0)

    def body(index, carry):
        rate_sum, input_sum, decay_sum = carry
        at = pl.multiple_of(index * chunk, chunk)
        window = pl.ds(at, chunk)
        grad = direct_ref[window, :] + shifted(value, at, chunk, 1)
        rate, gate = rate_ref[window, :], input_ref[window, :]
        conv = conv_ref[window, :].astype(F32)
        log_a = decay * rate
        decays = jnp.exp(log_a)
        root = jnp.sqrt(minus_expm1(2.0 * log_a))
        scale_grad = grad * conv
        log_grad = grad * shifted(states, at, chunk, 7) * mask_ref[window, 1:2] * decays
        log_grad = log_grad - scale_grad * gate * (decays * decays) / root
        rate_grad = (log_grad * decay * rate * (1.0 - rate)).astype(BF16)
        input_grad = (scale_grad * root * gate * (1.0 - gate)).astype(BF16)
        both[window, :width] = rate_grad
        both[window, width:] = input_grad
        conv_grad[window, :] = grad * root * gate
        return (
            rate_sum + fold(rate_grad.astype(F32)),
            input_sum + fold(input_grad.astype(F32)),
            decay_sum + fold(log_grad * rate),
        )

    rate_sum, input_sum, decay_sum = lax.fori_loop(0, rows // chunk, body, (zero, zero, zero))
    sums_ref[0:8, :] += rate_sum
    sums_ref[8:16, :] += input_sum
    sums_ref[16:24, :] += decay_sum * lean

    gate_part = dot_tn(conv_ref[...], both[...])

    @pl.when(first)
    def _():
        gate_grad_ref[...] = gate_part

    @pl.when(jnp.logical_not(first))
    def _():
        gate_grad_ref[...] += gate_part

    rounded = (conv_grad[0:rows, :] + dot_nt(both[...], gate_ref[...])).astype(BF16).astype(F32)
    conv_grad[0:rows, :] = rounded
    conv_grad[rows:, :] = jnp.zeros_like(conv_grad[rows:, :])
    head_ref[...] = rounded[0:8, :]

    def branch(at):
        window = pl.ds(at, chunk)
        total = jnp.zeros((chunk, width), F32)
        grad = conv_grad[window, :]
        sums_ref[24:32, :] += fold(grad)
        for tap in range(CONV):
            total = total + vec_ref[tap : tap + 1, :] * shifted(conv_grad, at, chunk, tap) * ahead_ref[
                window, tap : tap + 1
            ]
            behind = shifted(ext, at, chunk, 8 - tap) * mask_ref[window, tap : tap + 1]
            sums_ref[32 + 8 * tap : 40 + 8 * tap, :] += fold(grad * behind)
        branch_ref[window, :] = total.astype(BF16)
        tail_ref[...] = total[chunk - 8 :, :]

    chunked(rows, chunk, branch)


def backward_call(
    direct, coef, value, enter, states, before, rate, gate, conv, x_branch, edge, masks, ahead, vectors, gates
):
    count, rows, width = direct.shape
    seq = lambda *tail: pl.BlockSpec((None, *tail), lambda i: (i, 0, 0))
    whole = lambda *shape: pl.BlockSpec(shape, lambda i: (0, 0))
    return pl.pallas_call(
        backward_kernel,
        grid=(count,),
        in_specs=[
            seq(rows, width), seq(rows, width), seq(rows, width), seq(8, width),
            seq(rows, width), seq(8, width), seq(rows, width), seq(rows, width), seq(rows, width),
            seq(rows, width), seq(8, width), seq(rows, LANES), seq(rows, LANES),
            whole(8, width), whole(width, 2 * width),
        ],
        out_specs=[
            seq(rows, width), seq(8, width), seq(8, width), whole(64, width), whole(width, 2 * width)
        ],
        out_shape=[
            jax.ShapeDtypeStruct((count, rows, width), BF16),
            jax.ShapeDtypeStruct((count, 8, width), F32),
            jax.ShapeDtypeStruct((count, 8, width), F32),
            jax.ShapeDtypeStruct((64, width), F32),
            jax.ShapeDtypeStruct((width, 2 * width), F32),
        ],
        scratch_shapes=[
            pltpu.VMEM((rows + 8, width), F32),
            pltpu.VMEM((rows + 8, width), F32),
            pltpu.VMEM((rows + 8, width), F32),
            pltpu.VMEM((rows, 2 * width), BF16),
            pltpu.VMEM((rows + 8, width), F32),
        ],
        cost_estimate=pl.CostEstimate(
            flops=8 * count * rows * width * width,
            bytes_accessed=count * rows * width * 34,
            transcendentals=count * rows * width * 4,
        ),
        name="gates_backward",
    )(direct, coef, value, enter, states, before, rate, gate, conv, x_branch, edge, masks, ahead, vectors, gates)


def block_diagonal(rate_gate, input_gate, padded):
    heads, size, _ = rate_gate.shape

    def spread(gate):
        rows = [
            jnp.pad(gate[head], ((0, 0), (head * size, padded - (head + 1) * size)))
            for head in range(heads)
        ]
        rows.append(jnp.zeros((padded - heads * size, padded), gate.dtype))
        return jnp.concatenate(rows, axis=0)

    return jnp.concatenate([spread(rate_gate), spread(input_gate)], axis=1)


def shards(
    block_in, seg_ids, out_cot, norm_gain, mid_gain, gelu_proj, scan_proj, out_proj, gate_proj,
    up_proj, down_proj, conv_kernel, conv_bias, rate_gate, input_gate, rate_bias, input_bias,
    decay_param,
):
    seq_count, tok_count, part_width = block_in.shape
    row_count = seq_count * tok_count
    rec_width = gelu_proj.shape[1]
    hidden_width = gate_proj.shape[1]
    heads, size, _ = rate_gate.shape
    padded = -(-rec_width // LANES) * LANES
    extra = padded - rec_width

    def widen(value):
        return jnp.pad(value, ((0, 0), (0, extra)))

    def split(value):
        return value.reshape(seq_count, tok_count, value.shape[-1])

    x_full = lax.all_gather(block_in.reshape(row_count, part_width), "tp", axis=1, tiled=True)
    gains = lax.all_gather(jnp.stack([norm_gain, mid_gain]), "tp", axis=1, tiled=True).astype(F32)
    gain_one, gain_two = gains[0:1], gains[1:2]
    full_width = x_full.shape[1]

    w_in = gather_rows(jnp.concatenate([widen(gelu_proj), widen(scan_proj)], axis=1))
    w_out = gather_rows(widen(out_proj.T))
    w_ff = gather_rows(jnp.concatenate([gate_proj, up_proj], axis=1))
    w_down = gather_rows(down_proj.T)

    margin = CONV - 1
    start_tok = lax.axis_index("ctx") * tok_count
    padded_ids = jnp.concatenate(
        [
            jnp.full((seq_count, margin), -1, jnp.int32),
            seg_ids,
            jnp.full((seq_count, margin), -2, jnp.int32),
        ],
        axis=1,
    )
    ids = lax.dynamic_slice_in_dim(padded_ids, start_tok, tok_count + 2 * margin, 1)
    own_ids = ids[:, margin : margin + tok_count]
    back = [ids[:, margin - k : margin - k + tok_count] == own_ids for k in range(CONV)]
    ahead = [ids[:, margin + k : margin + k + tok_count] == own_ids for k in range(CONV)]
    fill = ((0, 0), (0, 0), (0, LANES - CONV))
    back = jnp.pad(jnp.stack(back, axis=-1).astype(F32), fill)
    ahead_f = jnp.stack(ahead, axis=-1).astype(F32)
    ahead = jnp.pad(ahead_f, fill)

    vectors = widen(
        jnp.concatenate(
            [conv_kernel, conv_bias[None], rate_bias[None], input_bias[None], decay_param[None]], axis=0
        )
    )
    gates = block_diagonal(rate_gate, input_gate, padded)

    x_rows = x_full.astype(F32)
    scale_one = lax.rsqrt(jnp.mean(x_rows * x_rows, axis=-1, keepdims=True) + EPS)
    normed = (x_rows * scale_one * gain_one).astype(BF16)
    y_pre = split(dot_nn(normed, w_in[:, :padded]))
    x_branch = split(dot_nn(normed, w_in[:, padded:]).astype(BF16))

    prev_edge = from_behind(x_branch[:, tok_count - margin :, :], "ctx", 1)
    edge = jnp.pad(prev_edge, ((0, 0), (8 - margin, 0), (0, 0)))
    conv, rate, gate, coef, local = forward_call(x_branch, edge, back, vectors, gates)
    state_in = entering(coef[:, -1], local[:, -1], False)
    states = local + coef * state_in[:, None, :]
    y_act, _ = gelu_parts(y_pre)
    mixed_in = (states * y_act).astype(BF16).reshape(row_count, padded)

    rec_part = dot_nt(mixed_in, w_out).astype(BF16)
    rec_own = lax.psum_scatter(rec_part, "tp", scatter_dimension=1, tiled=True)
    mid_own = block_in.reshape(row_count, part_width).astype(F32) + rec_own.astype(F32)
    mid = lax.all_gather(mid_own.astype(BF16), "tp", axis=1, tiled=True).astype(F32)
    scale_two = lax.rsqrt(jnp.mean(mid * mid, axis=-1, keepdims=True) + EPS)
    normed_mid = (mid * scale_two * gain_two).astype(BF16)

    cot = out_cot.reshape(row_count, full_width)
    hid_grad = dot_nn(cot, w_down)
    pre = dot_nn(normed_mid, w_ff)
    gate_pre, up_pre = pre[:, :hidden_width], pre[:, hidden_width:]
    gate_act, gate_slope = gelu_parts(gate_pre)
    hidden = (gate_act * up_pre).astype(BF16)
    both_grad = jnp.concatenate(
        [(hid_grad * up_pre * gate_slope).astype(BF16), (hid_grad * gate_act).astype(BF16)], axis=1
    )
    mid_part = dot_nt(both_grad, w_ff)
    weighted = mid_part * gain_two
    mean_two = jnp.mean(weighted * mid, axis=-1, keepdims=True)
    back_two = (scale_two * weighted - mid * (scale_two * scale_two * scale_two * mean_two)).astype(BF16)
    gain_two_part = jnp.sum(mid_part * mid * scale_two, axis=0)
    back_own = lax.psum_scatter(back_two, "tp", scatter_dimension=1, tiled=True)
    col_start = lax.axis_index("tp") * part_width
    cot_own = lax.dynamic_slice_in_dim(cot, col_start, part_width, 1).astype(F32)
    mid_grad_own = cot_own + back_own.astype(F32)
    rec_grad = lax.all_gather(mid_grad_own.astype(BF16), "tp", axis=1, tiled=True)

    mlp_part = dot_nt(hidden, w_down).astype(BF16)
    grad_down = scatter_rows(dot_tn(cot, hidden).astype(BF16))
    grad_ff = scatter_rows(dot_tn(normed_mid, both_grad).astype(BF16))
    mlp_own = lax.psum_scatter(mlp_part, "tp", scatter_dimension=1, tiled=True)
    block_out = split((mid_own + mlp_own.astype(F32)).astype(BF16))

    mixed_grad = split(dot_nn(rec_grad, w_out))
    grad_out = scatter_rows(dot_tn(rec_grad, mixed_in).astype(BF16))
    y_grad, direct, tail_coef, tail_value = reverse_call(mixed_grad, y_pre, states, rate, back, vectors)
    enter = entering(tail_coef[:, 0], tail_value[:, 0], True)
    rows_of = lambda value: jnp.broadcast_to(value[:, None, :], (seq_count, 8, padded))
    branch, tail, head, sums, gate_grad = backward_call(
        direct, tail_coef, tail_value, rows_of(enter), states, rows_of(state_in), rate, gate, conv,
        x_branch, edge, back, ahead, vectors, gates,
    )
    next_edge = from_behind(head[:, :margin].astype(BF16), "ctx", -1).astype(F32)
    lead = jnp.concatenate([next_edge, jnp.zeros((seq_count, 8, padded), F32)], axis=1)
    for tap in range(1, CONV):
        reach = jnp.pad(lead[:, :tap], ((0, 0), (8 - tap, 0), (0, 0)))
        tail = tail + vectors[tap] * reach * ahead_f[:, tok_count - 8 :, tap : tap + 1]
    branch = lax.dynamic_update_slice(branch, tail.astype(BF16), (0, tok_count - 8, 0))
    in_grad = jnp.concatenate(
        [y_grad.reshape(row_count, padded), branch.reshape(row_count, padded)], axis=1
    )
    in_part = dot_nt(in_grad, w_in)
    weighted = in_part * gain_one
    mean_one = jnp.mean(weighted * x_rows, axis=-1, keepdims=True)
    back_one = (scale_one * weighted - x_rows * (scale_one * scale_one * scale_one * mean_one)).astype(BF16)
    gain_one_part = jnp.sum(in_part * x_rows * scale_one, axis=0)
    in_own = lax.psum_scatter(back_one, "tp", scatter_dimension=1, tiled=True)
    grad_in = split(mid_grad_own + in_own.astype(F32))
    grad_in_w = scatter_rows(dot_tn(normed, in_grad).astype(BF16))

    gain_parts = lax.psum_scatter(
        jnp.stack([gain_one_part, gain_two_part]), "tp", scatter_dimension=1, tiled=True
    )
    sums = sums.reshape(8, 8, padded).sum(axis=1)
    gain_parts = jnp.pad(gain_parts, ((0, 0), (0, padded - part_width)))
    small = total_over_tokens(jnp.concatenate([sums, gain_parts], axis=0))

    def diagonal(value, column):
        return jnp.stack(
            [
                value[h * size : (h + 1) * size, column + h * size : column + (h + 1) * size]
                for h in range(heads)
            ]
        )

    pieces = jnp.concatenate([diagonal(gate_grad, 0), diagonal(gate_grad, padded)], axis=2)
    pieces = total_over_tokens(pieces)

    return (
        block_out,
        grad_in,
        small[8, :part_width],
        small[9, :part_width],
        grad_in_w[:, :rec_width],
        grad_in_w[:, padded : padded + rec_width],
        grad_out[:, :rec_width].T,
        grad_ff[:, :hidden_width],
        grad_ff[:, hidden_width:],
        grad_down.T,
        small[4:8, :rec_width],
        small[3, :rec_width],
        pieces[:, :, :size],
        pieces[:, :, size:],
        small[0, :rec_width],
        small[1, :rec_width],
        small[2, :rec_width],
    )


def solution(mesh):
    rows, columns = P(("fsdp", "ctx"), "tp"), P("tp", ("fsdp", "ctx"))
    stream, vector, gate = P("fsdp", "ctx", "tp"), P("tp"), P("tp", None, None)
    in_specs = (
        stream, P("fsdp", None), P("fsdp", "ctx", None), vector, vector, rows, rows, columns, rows, rows,
        columns, P(None, "tp"), vector, gate, gate, vector, vector, vector,
    )
    out_specs = (
        stream, stream, vector, vector, rows, rows, columns, rows, rows, columns, P(None, "tp"), vector,
        gate, gate, vector, vector, vector,
    )
    return jax.shard_map(shards, mesh=mesh, in_specs=in_specs, out_specs=out_specs, check_vma=False)
```

```python
import jax
import jax.numpy as jnp
from jax import lax
from jax.experimental import pallas as pl
from jax.experimental.layout import Layout, with_layout_constraint
from jax.experimental.pallas import tpu as pltpu
from jax.sharding import PartitionSpec as P

CONV = 4
EPS = 1e-06
LANES = 128
SEGS = 8
F32 = jnp.float32
BF16 = jnp.bfloat16


def xor_permute(value, axis, bit):
    count = lax.axis_size(axis)
    return lax.ppermute(value, axis, [(i, i ^ bit) for i in range(count)])


def quad_mesh():
    return lax.axis_size("fsdp") == 2 and lax.axis_size("ctx") == 4


def own_place():
    place = lax.axis_index("ctx")
    return lax.axis_index("fsdp"), place // 2, place % 2


def gather_rows(shard):
    rows, width = shard.shape
    if not quad_mesh():
        return lax.all_gather(shard, ("fsdp", "ctx"), axis=0, tiled=True)
    half = rows // 2
    own_x, own_y, own_c = own_place()
    from_x = xor_permute(shard, "fsdp", 1)
    from_y = xor_permute(shard, "ctx", 2)
    corner = jnp.concatenate(
        [xor_permute(from_y[:half], "fsdp", 1), xor_permute(from_x[half:], "ctx", 2)], axis=0
    )
    quad = [
        jnp.where(
            own_x == x, jnp.where(own_y == y, shard, from_y), jnp.where(own_y == y, from_x, corner)
        )
        for x in range(2)
        for y in range(2)
    ]
    quad = jnp.concatenate(quad, axis=0).reshape(4, 1, rows, width)
    other = xor_permute(quad, "ctx", 1)
    full = jnp.zeros((4, 2, rows, width), shard.dtype)
    full = lax.dynamic_update_slice(full, quad, (0, own_c, 0, 0))
    full = lax.dynamic_update_slice(full, other, (0, 1 - own_c, 0, 0))
    return full.reshape(8 * rows, width)


def row_major(value):
    return with_layout_constraint(value, Layout(major_to_minor=tuple(range(value.ndim))))


def choose(options, index):
    value = options[0]
    for position, option in enumerate(options[1:], 1):
        value = jnp.where(index == position, option, value)
    return value


def shifted_permute(value, step):
    count = lax.axis_size("tp")
    return lax.ppermute(value, "tp", [(i, (i + step) % count) for i in range(count)])


def exchange(block_for):
    count, mine = lax.axis_size("tp"), lax.axis_index("tp")
    got = [shifted_permute(block_for(step), step) if step else block_for(0) for step in range(count)]
    return [choose([got[(at - source) % count] for at in range(count)], mine) for source in range(count)]


def pick(value, index, axis):
    return lax.dynamic_index_in_dim(value, index, axis, keepdims=False)


def add_low(left, right):
    return (left.astype(F32) + right.astype(F32)).astype(BF16)


def scatter_rows(partial):
    if not quad_mesh():
        return lax.psum_scatter(
            partial, ("fsdp", "ctx"), scatter_dimension=0, tiled=True
        ).astype(F32)
    total, width = partial.shape
    rows = total // 8
    half = rows // 2
    own_x, own_y, own_c = own_place()
    cube = partial.reshape(4, 2, rows, width)
    got = xor_permute(pick(cube, 1 - own_c, 1), "ctx", 1)
    quad = add_low(pick(cube, own_c, 1), got).reshape(2, 2, rows, width)
    top, low = quad[:, :, :half], quad[:, :, half:]
    top_got = xor_permute(pick(top, 1 - own_x, 0), "fsdp", 1)
    low_got = xor_permute(pick(low, 1 - own_y, 1), "ctx", 2)
    top = add_low(pick(top, own_x, 0), top_got)
    low = add_low(pick(low, own_y, 1), low_got)
    top_last = xor_permute(pick(top, 1 - own_y, 0), "ctx", 2)
    low_last = xor_permute(pick(low, 1 - own_x, 0), "fsdp", 1)
    top = pick(top, own_y, 0).astype(F32) + top_last.astype(F32)
    low = pick(low, own_x, 0).astype(F32) + low_last.astype(F32)
    return jnp.concatenate([top, low], axis=0)


def total_over_tokens(value):
    if not quad_mesh():
        return lax.psum(value, ("fsdp", "ctx"))
    value = value + xor_permute(value, "ctx", 1)
    value = value + xor_permute(value, "fsdp", 1)
    return value + xor_permute(value, "ctx", 2)


def from_behind(value, axis, steps):
    count = lax.axis_size(axis)
    leading, last = (max(0, -steps), min(count, count - steps))
    return lax.ppermute(value, axis, [(source, source + steps) for source in range(leading, last)])


def entering(coef, state, backward):
    count, mine = lax.axis_size("ctx"), lax.axis_index("ctx")
    both = lax.all_gather(jnp.stack([coef, state]), "ctx")
    total = jnp.zeros_like(state)
    for step in range(count - 1):
        position = count - 1 - step if backward else step
        before = position > mine if backward else position < mine
        total = jnp.where(before, both[position, 0] * total + both[position, 1], total)
    return total


def dot_nt(left, right):
    return lax.dot_general(left, right, (((1,), (1,)), ((), ())), preferred_element_type=F32)


def dot_tn(left, right):
    return lax.dot_general(left, right, (((0,), (0,)), ((), ())), preferred_element_type=F32)


def dot_nn(left, right):
    return jnp.dot(left, right, preferred_element_type=F32)


GELU_C = 0.7978845608028654
GELU_A = 0.044715


def gelu_parts(values):
    square = values * values
    tanh = jnp.tanh(GELU_C * values * (1.0 + GELU_A * square))
    act = 0.5 * values * (1.0 + tanh)
    slope = 0.5 * (1.0 + tanh) + 0.5 * values * (1.0 - tanh * tanh) * GELU_C * (
        1.0 + 3.0 * GELU_A * square
    )
    return act, slope


def minus_expm1(value):
    series = 1.0 / 40320.0
    for factor in (5040.0, 720.0, 120.0, 24.0, 6.0, 2.0, 1.0):
        series = series * value + 1.0 / factor
    return jnp.where(value > -0.5, -value * series, 1.0 - jnp.exp(value))


def softplus(value):
    return jnp.maximum(value, 0.0) + jnp.log1p(jnp.exp(-jnp.abs(value)))


def sigmoid(value):
    return 1.0 / (1.0 + jnp.exp(-value))


def chunked(total, size, body):
    def step(index, carry):
        body(pl.multiple_of(index * size, size))
        return carry

    lax.fori_loop(0, total // size, step, 0)


def scan_rows(coef_tiles, value_tiles, coef_ref, value_ref, backward):
    tiles, rows, lanes = value_tiles.shape
    part = rows // SEGS

    def step(index, carry):
        at = part - 1 - index if backward else index
        rows_at = pl.ds(at, SEGS, stride=part)
        out = []
        for tile, (coef_run, value_run) in enumerate(carry):
            coef = coef_tiles[tile, rows_at, :]
            value_run = coef * value_run + value_tiles[tile, rows_at, :]
            coef_run = coef * coef_run
            coef_tiles[tile, rows_at, :] = coef_run
            value_tiles[tile, rows_at, :] = value_run
            out.append((coef_run, value_run))
        return tuple(out)

    start = (jnp.ones((SEGS, lanes), F32), jnp.zeros((SEGS, lanes), F32))
    ends = lax.fori_loop(0, part, step, (start,) * tiles)
    order = list(range(SEGS))[::-1] if backward else list(range(SEGS))
    for tile, (coef_end, value_end) in enumerate(ends):
        columns = slice(tile * lanes, (tile + 1) * lanes)
        coef_in, value_in = jnp.ones((1, lanes), F32), jnp.zeros((1, lanes), F32)
        for seg in order:
            window = pl.ds(seg * part, part)
            coef = coef_tiles[tile, window, :]
            value_ref[window, columns] = value_tiles[tile, window, :] + coef * value_in
            coef_ref[window, columns] = coef * coef_in
            value_in = coef_end[seg : seg + 1] * value_in + value_end[seg : seg + 1]
            coef_in = coef_end[seg : seg + 1] * coef_in


def shifted(ref, at, count, offset):
    if offset % 8 == 0:
        return ref[pl.ds(at + offset, count), :]
    return ref[pl.ds(at, count + 8), :][offset : offset + count]


def put_tiles(tiles_ref, window, value):
    for tile in range(tiles_ref.shape[0]):
        tiles_ref[tile, window, :] = value[:, tile * LANES : (tile + 1) * LANES]


def forward_kernel(
    x_ref, edge_ref, mask_ref, vec_ref, gate_ref,
    conv_ref, rate_ref, input_ref, coef_ref, state_ref,
    ext, pre, coef_tiles, value_tiles,
):
    rows, width = x_ref.shape
    ext[0:8, :] = edge_ref[...].astype(F32)
    ext[8:, :] = x_ref[...].astype(F32)
    chunk = 32

    def conv(at):
        total = vec_ref[4:5, :]
        for tap in range(CONV):
            total = total + vec_ref[tap : tap + 1, :] * shifted(ext, at, chunk, 8 - tap) * mask_ref[
                pl.ds(at, chunk), tap : tap + 1
            ]
        conv_ref[pl.ds(at, chunk), :] = total.astype(BF16)

    chunked(rows, chunk, conv)
    pre[...] = dot_nn(conv_ref[...], gate_ref[...])
    decay = -8.0 * softplus(vec_ref[7:8, :])

    def gates(at):
        window = pl.ds(at, chunk)
        rate = sigmoid(pre[window, :width] + vec_ref[5:6, :])
        gate = sigmoid(pre[window, width:] + vec_ref[6:7, :])
        log_a = decay * rate
        rate_ref[window, :] = rate
        input_ref[window, :] = gate
        put_tiles(coef_tiles, window, jnp.exp(log_a) * mask_ref[window, 1:2])
        put_tiles(
            value_tiles, window, jnp.sqrt(minus_expm1(2.0 * log_a)) * gate * conv_ref[window, :].astype(F32)
        )

    chunked(rows, chunk, gates)
    scan_rows(coef_tiles, value_tiles, coef_ref, state_ref, False)


def forward_call(x_branch, edge, masks, vectors, gates):
    count, rows, width = x_branch.shape
    seq = lambda *tail: pl.BlockSpec((None, *tail), lambda i: (i, 0, 0))
    whole = lambda *shape: pl.BlockSpec(shape, lambda i: (0, 0))
    wide = jax.ShapeDtypeStruct((count, rows, width), F32)
    return pl.pallas_call(
        forward_kernel,
        grid=(count,),
        in_specs=[
            seq(rows, width), seq(8, width), seq(rows, LANES), whole(8, width), whole(width, 2 * width)
        ],
        out_specs=[seq(rows, width)] * 5,
        out_shape=[jax.ShapeDtypeStruct((count, rows, width), BF16), wide, wide, wide, wide],
        scratch_shapes=[
            pltpu.VMEM((rows + 8, width), F32),
            pltpu.VMEM((rows, 2 * width), F32),
            pltpu.VMEM((width // LANES, rows, LANES), F32),
            pltpu.VMEM((width // LANES, rows, LANES), F32),
        ],
        cost_estimate=pl.CostEstimate(
            flops=4 * count * rows * width * width,
            bytes_accessed=count * rows * width * 20,
            transcendentals=count * rows * width * 6,
        ),
        name="conv_gates_scan",
    )(x_branch, edge, masks, vectors, gates)


def reverse_kernel(
    grad_ref, y_ref, state_ref, rate_ref, mask_ref, vec_ref, y_grad_ref, direct_ref, coef_ref, value_ref,
    coef_tiles, value_tiles,
):
    rows, width = grad_ref.shape
    decay = -8.0 * softplus(vec_ref[7:8, :])

    def body(at):
        window = pl.ds(at, 32)
        act, slope = gelu_parts(y_ref[window, :])
        grad = grad_ref[window, :].astype(F32)
        y_grad_ref[window, :] = (grad * state_ref[window, :] * slope).astype(BF16)
        direct = grad * act
        coef = jnp.exp(decay * rate_ref[window, :]) * mask_ref[window, 1:2]
        direct_ref[window, :] = direct
        put_tiles(coef_tiles, window, coef)
        put_tiles(value_tiles, window, coef * direct)

    chunked(rows, 32, body)
    scan_rows(coef_tiles, value_tiles, coef_ref, value_ref, True)


def reverse_call(grad, y_pre, states, rate, masks, vectors):
    count, rows, width = grad.shape
    seq = lambda *tail: pl.BlockSpec((None, *tail), lambda i: (i, 0, 0))
    whole = lambda *shape: pl.BlockSpec(shape, lambda i: (0, 0))
    wide = jax.ShapeDtypeStruct((count, rows, width), F32)
    return pl.pallas_call(
        reverse_kernel,
        grid=(count,),
        in_specs=[seq(rows, width)] * 4 + [seq(rows, LANES), whole(8, width)],
        out_specs=[seq(rows, width)] * 4,
        out_shape=[jax.ShapeDtypeStruct((count, rows, width), BF16), wide, wide, wide],
        scratch_shapes=[pltpu.VMEM((width // LANES, rows, LANES), F32)] * 2,
        cost_estimate=pl.CostEstimate(
            flops=40 * count * rows * width,
            bytes_accessed=count * rows * width * 30,
            transcendentals=count * rows * width * 2,
        ),
        name="reverse_scan",
    )(grad, y_pre, states, rate, masks, vectors)


def backward_kernel(
    direct_ref, coef_ref, value_ref, enter_ref, state_ref, before_ref, rate_ref, input_ref, conv_ref,
    x_ref, edge_ref, mask_ref, ahead_ref, vec_ref, gate_ref,
    branch_ref, tail_ref, head_ref, sums_ref, gate_grad_ref,
    ext, states, value, both, conv_grad,
):
    rows, width = direct_ref.shape
    chunk = 32
    decay = -8.0 * softplus(vec_ref[7:8, :])
    lean = -8.0 * sigmoid(vec_ref[7:8, :])
    first = pl.program_id(0) == 0

    ext[0:8, :] = edge_ref[...].astype(F32)
    ext[8:, :] = x_ref[...].astype(F32)
    states[7:8, :] = before_ref[0:1, :]
    states[8:, :] = state_ref[...]
    value[0:rows, :] = value_ref[...] + coef_ref[...] * enter_ref[0:1, :]
    value[rows : rows + 1, :] = enter_ref[0:1, :]

    @pl.when(first)
    def _():
        sums_ref[...] = jnp.zeros_like(sums_ref)

    zero = jnp.zeros((8, width), F32)

    def fold(array):
        return array.reshape(chunk // 8, 8, width).sum(axis=0)

    def body(index, carry):
        rate_sum, input_sum, decay_sum = carry
        at = pl.multiple_of(index * chunk, chunk)
        window = pl.ds(at, chunk)
        grad = direct_ref[window, :] + shifted(value, at, chunk, 1)
        rate, gate = rate_ref[window, :], input_ref[window, :]
        conv = conv_ref[window, :].astype(F32)
        log_a = decay * rate
        decays = jnp.exp(log_a)
        root = jnp.sqrt(minus_expm1(2.0 * log_a))
        scale_grad = grad * conv
        log_grad = grad * shifted(states, at, chunk, 7) * mask_ref[window, 1:2] * decays
        log_grad = log_grad - scale_grad * gate * (decays * decays) / root
        rate_grad = (log_grad * decay * rate * (1.0 - rate)).astype(BF16)
        input_grad = (scale_grad * root * gate * (1.0 - gate)).astype(BF16)
        both[window, :width] = rate_grad
        both[window, width:] = input_grad
        conv_grad[window, :] = grad * root * gate
        return (
            rate_sum + fold(rate_grad.astype(F32)),
            input_sum + fold(input_grad.astype(F32)),
            decay_sum + fold(log_grad * rate),
        )

    rate_sum, input_sum, decay_sum = lax.fori_loop(0, rows // chunk, body, (zero, zero, zero))
    sums_ref[0:8, :] += rate_sum
    sums_ref[8:16, :] += input_sum
    sums_ref[16:24, :] += decay_sum * lean

    gate_part = dot_tn(conv_ref[...], both[...])

    @pl.when(first)
    def _():
        gate_grad_ref[...] = gate_part

    @pl.when(jnp.logical_not(first))
    def _():
        gate_grad_ref[...] += gate_part

    rounded = (conv_grad[0:rows, :] + dot_nt(both[...], gate_ref[...])).astype(BF16).astype(F32)
    conv_grad[0:rows, :] = rounded
    conv_grad[rows:, :] = jnp.zeros_like(conv_grad[rows:, :])
    head_ref[...] = rounded[0:8, :]

    def branch(at):
        window = pl.ds(at, chunk)
        total = jnp.zeros((chunk, width), F32)
        grad = conv_grad[window, :]
        sums_ref[24:32, :] += fold(grad)
        for tap in range(CONV):
            total = total + vec_ref[tap : tap + 1, :] * shifted(conv_grad, at, chunk, tap) * ahead_ref[
                window, tap : tap + 1
            ]
            behind = shifted(ext, at, chunk, 8 - tap) * mask_ref[window, tap : tap + 1]
            sums_ref[32 + 8 * tap : 40 + 8 * tap, :] += fold(grad * behind)
        branch_ref[window, :] = total.astype(BF16)
        tail_ref[...] = total[chunk - 8 :, :]

    chunked(rows, chunk, branch)


def backward_call(
    direct, coef, value, enter, states, before, rate, gate, conv, x_branch, edge, masks, ahead, vectors, gates
):
    count, rows, width = direct.shape
    seq = lambda *tail: pl.BlockSpec((None, *tail), lambda i: (i, 0, 0))
    whole = lambda *shape: pl.BlockSpec(shape, lambda i: (0, 0))
    return pl.pallas_call(
        backward_kernel,
        grid=(count,),
        in_specs=[
            seq(rows, width), seq(rows, width), seq(rows, width), seq(8, width),
            seq(rows, width), seq(8, width), seq(rows, width), seq(rows, width), seq(rows, width),
            seq(rows, width), seq(8, width), seq(rows, LANES), seq(rows, LANES),
            whole(8, width), whole(width, 2 * width),
        ],
        out_specs=[
            seq(rows, width), seq(8, width), seq(8, width), whole(64, width), whole(width, 2 * width)
        ],
        out_shape=[
            jax.ShapeDtypeStruct((count, rows, width), BF16),
            jax.ShapeDtypeStruct((count, 8, width), F32),
            jax.ShapeDtypeStruct((count, 8, width), F32),
            jax.ShapeDtypeStruct((64, width), F32),
            jax.ShapeDtypeStruct((width, 2 * width), F32),
        ],
        scratch_shapes=[
            pltpu.VMEM((rows + 8, width), F32),
            pltpu.VMEM((rows + 8, width), F32),
            pltpu.VMEM((rows + 8, width), F32),
            pltpu.VMEM((rows, 2 * width), BF16),
            pltpu.VMEM((rows + 8, width), F32),
        ],
        cost_estimate=pl.CostEstimate(
            flops=8 * count * rows * width * width,
            bytes_accessed=count * rows * width * 34,
            transcendentals=count * rows * width * 4,
        ),
        name="gates_backward",
    )(direct, coef, value, enter, states, before, rate, gate, conv, x_branch, edge, masks, ahead, vectors, gates)


def block_diagonal(rate_gate, input_gate, padded):
    heads, size, _ = rate_gate.shape

    def spread(gate):
        rows = [
            jnp.pad(gate[head], ((0, 0), (head * size, padded - (head + 1) * size)))
            for head in range(heads)
        ]
        rows.append(jnp.zeros((padded - heads * size, padded), gate.dtype))
        return jnp.concatenate(rows, axis=0)

    return jnp.concatenate([spread(rate_gate), spread(input_gate)], axis=1)


def shards(
    block_in, seg_ids, out_cot, norm_gain, mid_gain, gelu_proj, scan_proj, out_proj, gate_proj,
    up_proj, down_proj, conv_kernel, conv_bias, rate_gate, input_gate, rate_bias, input_bias,
    decay_param,
):
    seq_count, tok_count, part_width = block_in.shape
    row_count = seq_count * tok_count
    rec_width = gelu_proj.shape[1]
    hidden_width = gate_proj.shape[1]
    heads, size, _ = rate_gate.shape
    padded = -(-rec_width // LANES) * LANES
    group = lax.axis_size("tp")
    own_rows = row_count // group
    extra = padded - rec_width

    def widen(value):
        return jnp.pad(value, ((0, 0), (0, extra)))

    def split(value):
        return value.reshape(seq_count, tok_count, value.shape[-1])

    x_full = lax.all_gather(block_in.reshape(row_count, part_width), "tp", axis=1, tiled=True)
    gains = lax.all_gather(jnp.stack([norm_gain, mid_gain]), "tp", axis=1, tiled=True).astype(F32)
    gain_one, gain_two = gains[0:1], gains[1:2]
    full_width = x_full.shape[1]

    w_in = gather_rows(row_major(jnp.concatenate([widen(gelu_proj), widen(scan_proj)], axis=1)))
    w_down = gather_rows(row_major(down_proj.T))
    x_full, out_shard = lax.optimization_barrier((x_full, row_major(widen(out_proj.T))))
    w_out = gather_rows(jnp.concatenate(exchange(lambda step: out_shard), axis=1))
    w_ff = gather_rows(jnp.concatenate([gate_proj, up_proj], axis=1))

    margin = CONV - 1
    start_tok = lax.axis_index("ctx") * tok_count
    padded_ids = jnp.concatenate(
        [
            jnp.full((seq_count, margin), -1, jnp.int32),
            seg_ids,
            jnp.full((seq_count, margin), -2, jnp.int32),
        ],
        axis=1,
    )
    ids = lax.dynamic_slice_in_dim(padded_ids, start_tok, tok_count + 2 * margin, 1)
    own_ids = ids[:, margin : margin + tok_count]
    back = [ids[:, margin - k : margin - k + tok_count] == own_ids for k in range(CONV)]
    ahead = [ids[:, margin + k : margin + k + tok_count] == own_ids for k in range(CONV)]
    fill = ((0, 0), (0, 0), (0, LANES - CONV))
    back = jnp.pad(jnp.stack(back, axis=-1).astype(F32), fill)
    ahead_f = jnp.stack(ahead, axis=-1).astype(F32)
    ahead = jnp.pad(ahead_f, fill)

    vectors = widen(
        jnp.concatenate(
            [conv_kernel, conv_bias[None], rate_bias[None], input_bias[None], decay_param[None]], axis=0
        )
    )
    gates = block_diagonal(rate_gate, input_gate, padded)

    x_rows = x_full.astype(F32)
    scale_one = lax.rsqrt(jnp.mean(x_rows * x_rows, axis=-1, keepdims=True) + EPS)
    normed = (x_rows * scale_one * gain_one).astype(BF16)
    y_pre = split(dot_nn(normed, w_in[:, :padded]))
    x_branch = split(dot_nn(normed, w_in[:, padded:]).astype(BF16))

    prev_edge = from_behind(x_branch[:, tok_count - margin :, :], "ctx", 1)
    edge = jnp.pad(prev_edge, ((0, 0), (8 - margin, 0), (0, 0)))
    conv, rate, gate, coef, local = forward_call(x_branch, edge, back, vectors, gates)
    state_in = entering(coef[:, -1], local[:, -1], False)
    states = local + coef * state_in[:, None, :]
    y_act, _ = gelu_parts(y_pre)
    mixed_in = (states * y_act).astype(BF16).reshape(group, own_rows, padded)

    mine = lax.axis_index("tp")
    mixed = jnp.concatenate(
        exchange(lambda step: pick(mixed_in, lax.rem(mine + step, group), 0)), axis=1
    )
    own = lambda value: lax.dynamic_slice_in_dim(value, mine * own_rows, own_rows, 0)
    x_own = own(x_full).astype(F32)
    mid = x_own + dot_nt(mixed, w_out)
    scale_two = lax.rsqrt(jnp.mean(mid * mid, axis=-1, keepdims=True) + EPS)
    normed_mid = lax.all_gather((mid * scale_two * gain_two).astype(BF16), "tp", axis=0, tiled=True)
    here = (jnp.arange(group) == mine).astype(F32)[:, None, None]

    def with_own(part, value):
        total = part.reshape(group, own_rows, full_width) + here * value[None]
        return total.astype(BF16).reshape(row_count, full_width)

    cot = out_cot.reshape(row_count, full_width)
    hid_grad = dot_nn(cot, w_down)
    pre = dot_nn(normed_mid, w_ff)
    gate_pre, up_pre = pre[:, :hidden_width], pre[:, hidden_width:]
    gate_act, gate_slope = gelu_parts(gate_pre)
    hidden = (gate_act * up_pre).astype(BF16)
    both_grad = jnp.concatenate(
        [(hid_grad * up_pre * gate_slope).astype(BF16), (hid_grad * gate_act).astype(BF16)], axis=1
    )
    mid_part = dot_nt(both_grad, w_ff).astype(BF16)
    mid_norm_grad = lax.psum_scatter(mid_part, "tp", scatter_dimension=0, tiled=True)
    mlp_part = with_own(dot_nt(hidden, w_down), mid)
    mid_norm_grad, mlp_part = lax.optimization_barrier((mid_norm_grad, mlp_part))
    block_out = split(lax.psum_scatter(mlp_part, "tp", scatter_dimension=1, tiled=True))

    mid_norm_grad = mid_norm_grad.astype(F32)
    weighted = mid_norm_grad * gain_two
    mean_two = jnp.mean(weighted * mid, axis=-1, keepdims=True)
    mid_grad = (
        own(cot).astype(F32)
        + scale_two * weighted
        - mid * (scale_two * scale_two * scale_two * mean_two)
    )
    gain_two_part = jnp.sum(mid_norm_grad * mid * scale_two, axis=0)
    rec_grad = mid_grad.astype(BF16)
    mixed_grad_own = dot_nn(rec_grad, w_out).astype(BF16)
    by_heads = [mixed_grad_own[:, g * padded : (g + 1) * padded] for g in range(group)]
    mixed_grad = exchange(lambda step: choose(by_heads[step:] + by_heads[:step], mine))
    mixed_grad = split(jnp.concatenate(mixed_grad, axis=0))

    grad_down = scatter_rows(row_major(dot_tn(cot, hidden).astype(BF16)))
    grad_ff = scatter_rows(dot_tn(normed_mid, both_grad).astype(BF16))
    grad_out = scatter_rows(dot_tn(rec_grad, mixed).astype(BF16)).astype(BF16)
    by_heads_out = [grad_out[:, g * padded : (g + 1) * padded] for g in range(group)]
    grad_out = sum(
        part.astype(F32) for part in exchange(lambda step: choose(by_heads_out[step:] + by_heads_out[:step], mine))
    )

    y_grad, direct, tail_coef, tail_value = reverse_call(mixed_grad, y_pre, states, rate, back, vectors)
    enter = entering(tail_coef[:, 0], tail_value[:, 0], True)
    rows_of = lambda value: jnp.broadcast_to(value[:, None, :], (seq_count, 8, padded))
    branch, tail, head, sums, gate_grad = backward_call(
        direct, tail_coef, tail_value, rows_of(enter), states, rows_of(state_in), rate, gate, conv,
        x_branch, edge, back, ahead, vectors, gates,
    )
    next_edge = from_behind(head[:, :margin].astype(BF16), "ctx", -1).astype(F32)
    lead = jnp.concatenate([next_edge, jnp.zeros((seq_count, 8, padded), F32)], axis=1)
    for tap in range(1, CONV):
        reach = jnp.pad(lead[:, :tap], ((0, 0), (8 - tap, 0), (0, 0)))
        tail = tail + vectors[tap] * reach * ahead_f[:, tok_count - 8 :, tap : tap + 1]
    branch = lax.dynamic_update_slice(branch, tail.astype(BF16), (0, tok_count - 8, 0))
    in_grad = jnp.concatenate(
        [y_grad.reshape(row_count, padded), branch.reshape(row_count, padded)], axis=1
    )
    in_part = dot_nt(in_grad, w_in)
    weighted = in_part * gain_one
    mean_one = jnp.mean(weighted * x_rows, axis=-1, keepdims=True)
    back_one = scale_one * weighted - x_rows * (scale_one * scale_one * scale_one * mean_one)
    gain_one_part = jnp.sum(in_part * x_rows * scale_one, axis=0)
    in_total = lax.psum_scatter(with_own(back_one, mid_grad), "tp", scatter_dimension=1, tiled=True)
    grad_in = split(in_total.astype(F32))
    grad_in_w = scatter_rows(row_major(dot_tn(normed, in_grad).astype(BF16)))

    gain_parts = jnp.stack([gain_one_part, gain_two_part])
    by_features = [gain_parts[:, g * part_width : (g + 1) * part_width] for g in range(group)]
    gain_parts = sum(exchange(lambda step: choose(by_features[step:] + by_features[:step], mine)))
    sums = sums.reshape(8, 8, padded).sum(axis=1)
    gain_parts = jnp.pad(gain_parts, ((0, 0), (0, padded - part_width)))
    small = total_over_tokens(jnp.concatenate([sums, gain_parts], axis=0))

    def diagonal(value, column):
        return jnp.stack(
            [
                value[h * size : (h + 1) * size, column + h * size : column + (h + 1) * size]
                for h in range(heads)
            ]
        )

    pieces = jnp.concatenate([diagonal(gate_grad, 0), diagonal(gate_grad, padded)], axis=2)
    pieces = total_over_tokens(pieces)

    return (
        block_out,
        grad_in,
        small[8, :part_width],
        small[9, :part_width],
        grad_in_w[:, :rec_width],
        grad_in_w[:, padded : padded + rec_width],
        grad_out[:, :rec_width].T,
        grad_ff[:, :hidden_width],
        grad_ff[:, hidden_width:],
        grad_down.T,
        small[4:8, :rec_width],
        small[3, :rec_width],
        pieces[:, :, :size],
        pieces[:, :, size:],
        small[0, :rec_width],
        small[1, :rec_width],
        small[2, :rec_width],
    )


def solution(mesh):
    rows, columns = P(("fsdp", "ctx"), "tp"), P("tp", ("fsdp", "ctx"))
    stream, vector, gate = P("fsdp", "ctx", "tp"), P("tp"), P("tp", None, None)
    in_specs = (
        stream, P("fsdp", None), P("fsdp", "ctx", None), vector, vector, rows, rows, columns, rows, rows,
        columns, P(None, "tp"), vector, gate, gate, vector, vector, vector,
    )
    out_specs = (
        stream, stream, vector, vector, rows, rows, columns, rows, rows, columns, P(None, "tp"), vector,
        gate, gate, vector, vector, vector,
    )
    return jax.shard_map(shards, mesh=mesh, in_specs=in_specs, out_specs=out_specs, check_vma=False)
```
